1024 devices in a mesh: prow: 32 (over x, z_lo), pcol: 16 (over y, z_hi), layer: 2 (over core).
Axes of the slice: x: 8, y: 8, z: 8 (z_hi: 2, z_lo: 4; z = z_hi * 4 + z_lo), core: 2. Of those that a mesh axis runs over, the one named last changes fastest.
Arguments:
- p_vals: bfloat16 [512, 64, 1536], P(('prow', 'pcol'), None, 'layer'), may hold values from -2 to 2
- p_cols: int32 [512, 24], P(('prow', 'pcol'), 'layer'), may hold values from 0 to 511, as said below
- c_cols: int32 [512, 16, 6], P('prow', 'pcol'), may hold values from 0 to 511, as said below
Outputs:
- c_vals: bfloat16 [512, 16, 64, 384], P('prow', 'pcol', None, 'layer')
The draws below stay inside these ranges and needn't reach their ends.
Inputs may be any that keep to these rules, and one draw needn't show every extreme that they name: `p_cols`: the first 12 block columns of every row are even and the rest odd; within a row the 24 block columns are distinct. `c_cols`: for row i and group c the 6 columns are distinct and each column j has (j) % (16) == c.
All inputs are finite; a program needn't handle non-finite values.
Results may differ from the reference program's by a relative error of at most 0.002.
Values may be sent and summed in bfloat16 or wider, within the bound.
A program may use at most 32 MiB of HBM per device.

```python
import jax
import jax.numpy as jnp
from jax import lax

BS = 64
K = 24
BD = 1
NB = 512
TR = 16
NQ = 32
KC = 6


def shared_order(key):
    return jax.random.permutation(jax.random.fold_in(key, 7), NB).astype(jnp.int32)


def draw_p_cols(key, part):
    half_count = NB // 2
    hold = K // 2
    window = 2 * hold
    order = shared_order(key)
    noise = jax.random.randint(jax.random.fold_in(key, 11), (NB, 2, window), 0, 1 << 20)
    scores = noise * window + jnp.arange(window, dtype=jnp.int32)[None, None, :]
    best, offsets = lax.top_k(scores, hold)
    even_center = order // 2
    odd_center = order % half_count // 2
    center = jnp.stack([even_center, odd_center], axis=1)[:, :, None]
    halves = (center - hold + offsets.astype(jnp.int32)) % half_count
    parity = jnp.arange(2, dtype=jnp.int32)[None, :, None]
    return (2 * halves + parity).reshape(NB, K).astype(jnp.int32)


def draw_c_cols(key, part):
    group_count = TR // BD
    half_count = NB // 2
    order = shared_order(key)
    slots = jnp.arange(NQ, dtype=jnp.int32)
    group = jnp.arange(group_count, dtype=jnp.int32)
    columns = slots[None, :] // BD * TR + group[:, None] * BD + slots[None, :] % BD
    place_rows = order % half_count
    place_cols = jnp.take(order, columns.reshape(-1), axis=0).reshape(group_count, NQ) % half_count
    apart = jnp.abs(place_cols[None, :, :] - place_rows[:, None, None])
    distance = jnp.minimum(apart, half_count - apart)
    jitter = jax.random.randint(jax.random.fold_in(key, 13), (NB, group_count, NQ), 0, 4)
    scores = (distance + jitter) * NQ + slots[None, None, :]
    best, picks = lax.top_k(-scores, KC)
    picks = picks.astype(jnp.int32)
    picks = jnp.concatenate([picks[..., 0::2], picks[..., 1::2]], axis=-1)
    grid_group = group[None, :, None]
    return (picks // BD * TR + grid_group * BD + picks % BD).astype(jnp.int32)


def levels(own_key, shape, split, least, largest):
    def one(axis_at, shards_of):
        draws = jax.random.uniform(jax.random.fold_in(jax.random.fold_in(own_key, 6), axis_at), (shards_of,), jnp.float32, least / len(split), largest / len(split))
        return jnp.repeat(jnp.exp(draws), shape[axis_at] // shards_of).reshape((-1,) + (1,) * (len(shape) - axis_at - 1))

    loudness = one(*split[0])
    for cut in split[1:]:
        loudness = loudness * one(*cut)
    return loudness


def bell_draw(own_key, dims, deviation, reach, pieces=(), held_as=jnp.bfloat16):
    entries = deviation * jax.random.normal(own_key, dims, jnp.float32)
    if pieces:
        entries = entries * levels(own_key, dims, pieces, -0.22, 0.18)
    return jnp.clip(entries, -reach, reach).astype(held_as)


def setup_inputs(seed: int = 0) -> dict:
    splits = jax.random.split(jax.random.key(seed), 4)
    p_vals = bell_draw(splits[0], (NB, BS, K * BS), 0.35, 2.0, ((0, 512), (2, 2)))
    p_cols = draw_p_cols(jax.random.fold_in(splits[3], 71), 0)
    c_cols = draw_c_cols(jax.random.fold_in(splits[3], 71), 0)
    return dict(p_vals=p_vals, p_cols=p_cols, c_cols=c_cols)


def reference(p_vals, p_cols, c_cols):
    groups = c_cols.shape[1]

    def one_row(index):
        row_block = p_vals[index].astype(jnp.float32)
        row_index = p_cols[index]
        targets = c_cols[index].reshape(-1)
        total = targets.shape[0]
        picked = jnp.take(p_vals, targets, axis=0).astype(jnp.float32)
        picked_cols = jnp.take(p_cols, targets, axis=0)
        matched = (row_index[None, :, None] == picked_cols[:, None, :]).astype(jnp.float32)
        blocks = picked.reshape(total, BS, K, BS)
        chosen = jnp.einsum('mab,mybz->myaz', matched, blocks).astype(jnp.bfloat16)
        chosen = lax.optimization_barrier(chosen)
        chosen = chosen.astype(jnp.float32).reshape(total, BS, K * BS)
        product = jnp.einsum('xk,myk->xmy', row_block, chosen)
        product = product.reshape(BS, groups, KC * BS)
        return jnp.transpose(product, (1, 0, 2)).astype(jnp.bfloat16)

    return lax.map(one_row, jnp.arange(NB, dtype=jnp.int32))
```

```python
import jax
import jax.numpy as jnp
from jax import lax
from jax.experimental import pallas as pl
from jax.experimental.pallas import tpu as pltpu
from jax.sharding import PartitionSpec as P

MESH = pl.DeviceIdType.MESH
NX, NZ, NY, NH = 8, 4, 8, 2
COLS, ROWS = NX * NZ, NY * NH
LANES = 128


def gather_kernel(vals, cols, colv, colc, rowv, rowc, a_send, a_recv, b_send, b_recv, own_sem):
    me_p = lax.axis_index("prow")
    me_q = lax.axis_index("pcol")
    x, z = me_p // NZ, me_p % NZ
    y, h = me_q // NH, me_q % NH

    def on_p(dx, dz):
        return (x + dx + NX) % NX * NZ + (z + dz + NZ) % NZ

    def on_q(dy, dh):
        return (y + dy + NY) % NY * NH + (h + dh) % NH

    barrier = pltpu.get_barrier_semaphore()
    partners = [{"prow": on_p(0, k)} for k in range(1, NZ)]
    partners += [{"prow": on_p(1, 0)}, {"prow": on_p(-1, 0)}]
    partners += [{"pcol": on_q(0, 1)}, {"pcol": on_q(1, 0)}, {"pcol": on_q(-1, 0)}]
    for who in partners:
        pl.semaphore_signal(barrier, inc=1, device_id=who, device_id_type=MESH)
    pl.semaphore_wait(barrier, len(partners))

    def copies(dst_v, dst_c, slot, own, sends, recvs, sid, who):
        src_v = vals.at[0] if own else dst_v.at[slot]
        src_c = cols.at[0] if own else dst_c.at[slot]
        return [
            pltpu.make_async_remote_copy(
                src_ref=src,
                dst_ref=dst.at[slot],
                send_sem=sends.at[k, sid],
                recv_sem=recvs.at[k, sid],
                device_id=who,
                device_id_type=MESH,
            )
            for k, (src, dst) in enumerate(((src_c, dst_c), (src_v, dst_v)))
        ]

    sent = []

    def send_a(slot, own, sid, who):
        for c in copies(colv, colc, slot, own, a_send, a_recv, sid, {"prow": who}):
            c.start()
            sent.append(c)

    def send_b(slot, own, sid, who):
        for c in copies(rowv, rowc, slot, own, b_send, b_recv, sid, {"pcol": who}):
            c.start()
            sent.append(c)

    def recv_a(slot, sid):
        for c in copies(colv, colc, slot, False, a_send, a_recv, sid, {"prow": on_p(1, 0)}):
            c.wait_recv()

    def recv_b(slot, sid):
        for c in copies(rowv, rowc, slot, False, b_send, b_recv, sid, {"pcol": on_q(1, 0)}):
            c.wait_recv()

    def a_right(d, q):
        return NZ + (d - 1) * NZ + q

    def a_left(d, q):
        return NZ + (NX // 2) * NZ + (d - 1) * NZ + q

    def b_right(d, p):
        return 1 + (d - 1) * NH + p

    def b_left(d, p):
        return 1 + (NY // 2) * NH + (d - 1) * NH + p

    def forward_a(slot, own, d, q):
        if d < NX // 2 - 1 or q < NZ // 2:
            send_a(slot, own, a_right(d + 1, q), on_p(1, 0))

    def forward_a_left(slot, own, d, q):
        if d < NX // 2 - 1 or q >= NZ // 2:
            send_a(slot, own, a_left(d + 1, q), on_p(-1, 0))

    def forward_b(slot, own, d, p):
        if d < NY // 2 - 1 or p == 0:
            send_b(slot, own, b_right(d + 1, p), on_q(1, 0))

    def forward_b_left(slot, own, d, p):
        if d < NY // 2 - 1 or p == 1:
            send_b(slot, own, b_left(d + 1, p), on_q(-1, 0))

    forward_a(me_p, True, 0, 0)
    forward_a_left(me_p, True, 0, 0)
    forward_b(me_q, True, 0, 0)
    forward_b_left(me_q, True, 0, 0)
    for k in range(1, NZ):
        send_a(me_p, True, k, on_p(0, k))
    send_b(me_q, True, 0, on_q(0, 1))
    own_copies = [
        pltpu.make_async_copy(vals.at[0], colv.at[me_p], own_sem.at[0]),
        pltpu.make_async_copy(cols.at[0], colc.at[me_p], own_sem.at[1]),
        pltpu.make_async_copy(vals.at[0], rowv.at[me_q], own_sem.at[2]),
        pltpu.make_async_copy(cols.at[0], rowc.at[me_q], own_sem.at[3]),
    ]
    for c in own_copies:
        c.start()

    for q in range(1, NZ):
        recv_a(on_p(0, -q), q)
        forward_a(on_p(0, -q), False, 0, q)
        forward_a_left(on_p(0, -q), False, 0, q)
    recv_b(on_q(0, 1), 0)
    forward_b(on_q(0, 1), False, 0, 1)
    forward_b_left(on_q(0, 1), False, 0, 1)

    for d in range(1, NX // 2 + 1):
        last = d == NX // 2
        for q in range(NZ):
            if not last or q < NZ // 2:
                recv_a(on_p(-d, -q), a_right(d, q))
                if not last:
                    forward_a(on_p(-d, -q), False, d, q)
            if not last or q >= NZ // 2:
                recv_a(on_p(d, -q), a_left(d, q))
                if not last:
                    forward_a_left(on_p(d, -q), False, d, q)
            if q % 2 == 1:
                p = q // 2
                if not last or p == 0:
                    recv_b(on_q(-d, p), b_right(d, p))
                    if not last:
                        forward_b(on_q(-d, p), False, d, p)
                if not last or p == 1:
                    recv_b(on_q(d, p), b_left(d, p))
                    if not last:
                        forward_b_left(on_q(d, p), False, d, p)
    for c in own_copies:
        c.wait()
    for c in sent:
        c.wait_send()


def gather(vals, cols):
    n_a = NZ + NX * NZ
    n_b = 1 + NY * NH
    dma = pltpu.SemaphoreType.DMA
    shape = vals.shape[1:]
    return pl.pallas_call(
        gather_kernel,
        name="gather_both",
        out_shape=(
            jax.ShapeDtypeStruct((COLS,) + shape, vals.dtype),
            jax.ShapeDtypeStruct((COLS, 1, LANES), jnp.int32),
            jax.ShapeDtypeStruct((ROWS,) + shape, vals.dtype),
            jax.ShapeDtypeStruct((ROWS, 1, LANES), jnp.int32),
        ),
        in_specs=[pl.BlockSpec(memory_space=pltpu.VMEM)] * 2,
        out_specs=[pl.BlockSpec(memory_space=pl.ANY)] * 4,
        scratch_shapes=[dma((2, n_a)), dma((2, n_a)), dma((2, n_b)), dma((2, n_b)), dma((4,))],
        compiler_params=pltpu.CompilerParams(collective_id=0, has_side_effects=True),
    )(vals, cols)


def product_kernel(
    picks, rowv, colv, out, rows, stage, twice, chosen, own, send, recv, row_sem, col_sem, send_sem, recv_sem
):
    n_rows, edge, width = rows.shape
    slots = width // edge
    per_copy = COLS // col_sem.shape[0]
    groups = col_sem.shape[0]
    half = own.shape[2] // edge
    me = lax.axis_index("layer")
    other = {"layer": 1 - me}

    row_copy = pltpu.make_async_copy(rowv, rows, row_sem)
    col_copies = [
        pltpu.make_async_copy(
            colv.at[pl.ds(g * per_copy, per_copy)], stage.at[pl.ds(g * per_copy, per_copy)], col_sem.at[g]
        )
        for g in range(groups)
    ]
    for c in col_copies:
        c.start()
    row_copy.start()
    barrier = pltpu.get_barrier_semaphore()
    pl.semaphore_signal(barrier, inc=1, device_id=other, device_id_type=MESH)
    low = lax.broadcasted_iota(jnp.int32, (edge, LANES), 1) < edge
    twice[COLS * slots] = jnp.zeros((edge, LANES), twice.dtype)
    for g in range(groups):
        col_copies[g].wait()

        def spread(j, carry):
            for b in range(slots // 2):
                pair = stage[j, :, b * LANES : (b + 1) * LANES]
                turned = jnp.concatenate([pair[:, edge:], pair[:, :edge]], axis=1)
                twice[j * slots + 2 * b] = jnp.where(low, pair, turned)
                twice[j * slots + 2 * b + 1] = jnp.where(low, turned, pair)
            return carry

        lax.fori_loop(g * per_copy, (g + 1) * per_copy, spread, 0)
    row_copy.wait()
    pl.semaphore_wait(barrier, 1)

    def swap(i):
        return pltpu.make_async_remote_copy(
            src_ref=send.at[i],
            dst_ref=recv.at[i],
            send_sem=send_sem.at[i],
            recv_sem=recv_sem.at[i],
            device_id=other,
            device_id_type=MESH,
        )

    def one_row(i, carry):
        a = rows[i]
        for side, target in ((1, send), (0, own)):
            for o in range(half):
                for p in range(slots // 2):
                    at = (side * half + o) * slots + 2 * p
                    first = twice[picks[i, at]]
                    second = twice[picks[i, at + 1]]
                    chosen[side, o * edge : (o + 1) * edge, p * LANES : (p + 1) * LANES] = jnp.where(
                        low, first, second
                    )
            target[i] = lax.dot_general(
                a, chosen[side], (((1,), (1,)), ((), ())), preferred_element_type=jnp.float32
            )
            if side == 1:

                @pl.when(i > 0)
                def _():
                    swap(i - 1).start()

        return carry

    lax.fori_loop(0, n_rows, one_row, 0)
    swap(n_rows - 1).start()

    def finish(i, carry):
        swap(i).wait_recv()
        out[i, 0] = (own[i] + recv[i]).astype(out.dtype)
        return carry

    lax.fori_loop(0, n_rows, finish, 0)

    def drain(i, carry):
        swap(i).wait_send()
        return carry

    lax.fori_loop(0, n_rows, drain, 0)


def product(picks, rowv, colv, half):
    n_rows, edge, width = rowv.shape
    slots = width // edge
    groups = 8
    dma = pltpu.SemaphoreType.DMA
    share = (n_rows, edge, half * edge)
    return pl.pallas_call(
        product_kernel,
        name="pick_multiply_swap",
        out_shape=jax.ShapeDtypeStruct((n_rows, 1, edge, half * edge), rowv.dtype),
        in_specs=[
            pl.BlockSpec(memory_space=pltpu.SMEM),
            pl.BlockSpec(memory_space=pl.ANY),
            pl.BlockSpec(memory_space=pl.ANY),
        ],
        out_specs=pl.BlockSpec(memory_space=pltpu.VMEM),
        scratch_shapes=[
            pltpu.VMEM((n_rows, edge, width), rowv.dtype),
            pltpu.VMEM((COLS, edge, width), rowv.dtype),
            pltpu.VMEM((COLS * slots + 1, edge, LANES), rowv.dtype),
            pltpu.VMEM((2, half * edge, width), rowv.dtype),
            pltpu.VMEM(share, jnp.float32),
            pltpu.VMEM(share, jnp.float32),
            pltpu.VMEM(share, jnp.float32),
            dma(()),
            dma((groups,)),
            dma((n_rows,)),
            dma((n_rows,)),
        ],
        compiler_params=pltpu.CompilerParams(collective_id=1, has_side_effects=True),
    )(picks, rowv, colv)


def pick_table(row_cols, col_cols, targets):
    slots = row_cols.shape[1]
    count = col_cols.shape[0] * slots
    at = jnp.arange(count, dtype=jnp.int32)
    same = (targets[:, :, None, None] == (at // slots)[None, None, None, :]) & (
        row_cols[:, None, :, None] == col_cols.reshape(-1)[None, None, None, :]
    )
    found = count + jnp.sum(jnp.where(same, at - count, 0), axis=-1)
    return found.reshape(row_cols.shape[0], -1)


def per_device(p_vals, p_cols, c_cols):
    slots = p_cols.shape[1]
    half = c_cols.shape[2] // 2
    wanted = c_cols[:, 0, :] // ROWS
    targets = jnp.where(lax.axis_index("layer") == 0, wanted, jnp.roll(wanted, half, axis=1))
    padded = jnp.pad(p_cols[:, None, :], ((0, 0), (0, 0), (0, LANES - slots)))
    colv, colc, rowv, rowc = gather(p_vals, padded)
    picks = pick_table(rowc[:, 0, :slots], colc[:, 0, :slots], targets)
    return product(picks, rowv, colv, half)


def solution(mesh):
    return jax.shard_map(
        per_device,
        mesh=mesh,
        in_specs=(
            P(("prow", "pcol"), None, "layer"),
            P(("prow", "pcol"), "layer"),
            P("prow", "pcol", None),
        ),
        out_specs=P("prow", "pcol", None, "layer"),
        check_vma=False,
    )
```

```python
import jax
import jax.numpy as jnp
from jax import lax
from jax.experimental import pallas as pl
from jax.experimental.pallas import tpu as pltpu
from jax.sharding import PartitionSpec as P

MESH = pl.DeviceIdType.MESH
NX, NZ, NY, NH = 8, 4, 8, 2
COLS, ROWS = NX * NZ, NY * NH
LANES = 128


def gather_kernel(vals, cols, colv, colc, rowv, rowc, a_send, a_recv, b_send, b_recv, own_sem):
    me_p = lax.axis_index("prow")
    me_q = lax.axis_index("pcol")
    x, z = me_p // NZ, me_p % NZ
    y, h = me_q // NH, me_q % NH
    peer_z = (z, z + 1 - 2 * (z % 2), (z + 2) % NZ, NZ - 1 - z)

    def on_p(dx, q):
        return (x + dx + NX) % NX * NZ + peer_z[q]

    def on_q(dy, p):
        return (y + dy + NY) % NY * NH + (h + p) % NH

    barrier = pltpu.get_barrier_semaphore()
    partners = [{"prow": on_p(0, k)} for k in range(1, NZ)]
    partners += [{"prow": on_p(1, 0)}, {"prow": on_p(-1, 0)}]
    partners += [{"pcol": on_q(1, 0)}, {"pcol": on_q(-1, 0)}]
    partners += [{"prow": on_p(0, k), "pcol": on_q(0, 1)} for k in range(NZ)]
    for who in partners:
        pl.semaphore_signal(barrier, inc=1, device_id=who, device_id_type=MESH)
    pl.semaphore_wait(barrier, len(partners))

    def copies(pairs, sends, recvs, sid, who):
        return [
            pltpu.make_async_remote_copy(
                src_ref=src,
                dst_ref=dst,
                send_sem=sends.at[k, sid],
                recv_sem=recvs.at[k, sid],
                device_id=who,
                device_id_type=MESH,
            )
            for k, (src, dst) in enumerate(pairs)
        ]

    sent = []

    def copies_a(slot, own, sid, who):
        src_c, src_v = (cols.at[0], vals.at[0]) if own else (colc.at[slot], colv.at[slot])
        return copies(((src_c, colc.at[slot]), (src_v, colv.at[slot])), a_send, a_recv, sid, {"prow": who})

    def copies_b(slot, own, sid, who):
        src_c, src_v = (cols.at[0], vals.at[0]) if own else (rowc.at[slot], rowv.at[slot])
        return copies(((src_c, rowc.at[slot]), (src_v, rowv.at[slot])), b_send, b_recv, sid, {"pcol": who})

    def send_a(slot, own, sid, who):
        for c in copies_a(slot, own, sid, who):
            c.start()
            sent.append(c)

    def send_b(slot, own, sid, who):
        for c in copies_b(slot, own, sid, who):
            c.start()
            sent.append(c)

    def recv_a(slot, sid):
        for c in copies_a(slot, False, sid, on_p(1, 0)):
            c.wait_recv()

    def recv_b(slot, sid):
        for c in copies_b(slot, False, sid, on_q(1, 0)):
            c.wait_recv()

    half_x, half_y = NX // 2, NY // 2

    def a_id(way, d, q):
        return NZ + (way * half_x + d - 1) * NZ + q

    def b_id(way, d, p):
        return 1 + (way * half_y + d - 1) * NH + p

    def goes_a(way, d, q):
        return d < half_x or (q >= NZ // 2) == (way == 1)

    def goes_b(way, d, p):
        return d < half_y or p == way

    def forward_a(way, d, q, own=False):
        if goes_a(way, d + 1, q) and d < half_x:
            step = -1 if way else 1
            send_a(on_p(-step * d, q), own, a_id(way, d + 1, q), on_p(step, 0))

    def forward_b(way, d, p, own=False):
        if goes_b(way, d + 1, p) and d < half_y:
            step = -1 if way else 1
            send_b(on_q(-step * d, p), own, b_id(way, d + 1, p), on_q(step, 0))

    def take_a(d, q):
        if d == 0:
            recv_a(on_p(0, q), q)
        for way in (0, 1):
            if d > 0 and goes_a(way, d, q):
                recv_a(on_p(d if way else -d, q), a_id(way, d, q))
                forward_a(way, d, q)
            if d == 0:
                forward_a(way, 0, q)

    def take_b(d, p):
        if d == 0:
            recv_b(on_q(0, 1), 0)
        for way in (0, 1):
            if d > 0 and goes_b(way, d, p):
                recv_b(on_q(d if way else -d, p), b_id(way, d, p))
                forward_b(way, d, p)
            if d == 0:
                forward_b(way, 0, p)

    edge = z % (NZ - 1) == 0

    def cross(q):
        @pl.when(edge)
        def _():
            for k, (src, dst) in enumerate(
                ((colc.at[on_p(0, q)], rowc.at[me_q]), (colv.at[on_p(0, q)], rowv.at[me_q]))
            ):
                cross_copy(q, k, src, dst).start()

    def cross_copy(q, k, src, dst):
        return pltpu.make_async_remote_copy(
            src_ref=src,
            dst_ref=dst,
            send_sem=own_sem.at[4 + 2 * (q - 2) + k],
            recv_sem=b_recv.at[k, 0],
            device_id={"prow": on_p(0, q), "pcol": on_q(0, 1)},
            device_id_type=MESH,
        )

    for q in range(1, NZ):
        send_a(me_p, True, q, on_p(0, q))
    for way in (0, 1):
        forward_a(way, 0, 0, True)
        forward_b(way, 0, 0, True)
    own_copies = [
        pltpu.make_async_copy(vals.at[0], colv.at[me_p], own_sem.at[0]),
        pltpu.make_async_copy(cols.at[0], colc.at[me_p], own_sem.at[1]),
        pltpu.make_async_copy(vals.at[0], rowv.at[me_q], own_sem.at[2]),
        pltpu.make_async_copy(cols.at[0], rowc.at[me_q], own_sem.at[3]),
    ]
    for c in own_copies:
        c.start()

    take_a(1, 0)
    take_b(1, 0)
    take_a(0, 1)
    take_a(2, 0)
    take_b(2, 0)
    take_a(0, 2)
    cross(2)
    take_a(1, 1)
    take_a(0, 3)
    cross(3)
    take_a(1, 2)
    take_a(2, 1)
    take_b(3, 0)
    take_b(0, 1)
    take_a(3, 0)
    take_a(1, 3)
    take_b(1, 1)
    take_b(4, 0)
    take_a(2, 2)
    take_a(3, 1)
    take_b(2, 1)
    take_a(2, 3)
    take_a(4, 0)
    take_a(3, 2)
    take_b(3, 1)
    take_a(4, 1)
    take_a(3, 3)
    take_a(4, 2)
    take_b(4, 1)
    take_a(4, 3)
    for c in own_copies:
        c.wait()
    for c in sent:
        c.wait_send()

    @pl.when(edge)
    def _():
        for q in (2, 3):
            for k, (src, dst) in enumerate(
                ((colc.at[on_p(0, q)], rowc.at[me_q]), (colv.at[on_p(0, q)], rowv.at[me_q]))
            ):
                cross_copy(q, k, src, dst).wait_send()


def gather(vals, cols):
    n_a = NZ + NX * NZ
    n_b = 1 + NY * NH
    dma = pltpu.SemaphoreType.DMA
    shape = vals.shape[1:]
    return pl.pallas_call(
        gather_kernel,
        name="gather_both",
        out_shape=(
            jax.ShapeDtypeStruct((COLS,) + shape, vals.dtype),
            jax.ShapeDtypeStruct((COLS, 1, LANES), jnp.int32),
            jax.ShapeDtypeStruct((ROWS,) + shape, vals.dtype),
            jax.ShapeDtypeStruct((ROWS, 1, LANES), jnp.int32),
        ),
        in_specs=[pl.BlockSpec(memory_space=pltpu.VMEM)] * 2,
        out_specs=[pl.BlockSpec(memory_space=pl.ANY)] * 4,
        scratch_shapes=[dma((2, n_a)), dma((2, n_a)), dma((2, n_b)), dma((2, n_b)), dma((8,))],
        compiler_params=pltpu.CompilerParams(collective_id=0, has_side_effects=True),
    )(vals, cols)


def product_kernel(
    picks, rowv, colv, out, rows, stage, twice, chosen, own, send, recv, row_sem, col_sem, send_sem, recv_sem
):
    n_rows, edge, width = rows.shape
    slots = width // edge
    per_copy = COLS // col_sem.shape[0]
    groups = col_sem.shape[0]
    half = own.shape[2] // edge
    me = lax.axis_index("layer")
    other = {"layer": 1 - me}

    row_copy = pltpu.make_async_copy(rowv, rows, row_sem)
    col_copies = [
        pltpu.make_async_copy(
            colv.at[pl.ds(g * per_copy, per_copy)], stage.at[pl.ds(g * per_copy, per_copy)], col_sem.at[g]
        )
        for g in range(groups)
    ]
    for c in col_copies:
        c.start()
    row_copy.start()
    barrier = pltpu.get_barrier_semaphore()
    pl.semaphore_signal(barrier, inc=1, device_id=other, device_id_type=MESH)
    low = lax.broadcasted_iota(jnp.int32, (edge, LANES), 1) < edge
    twice[COLS * slots] = jnp.zeros((edge, LANES), twice.dtype)
    for g in range(groups):
        col_copies[g].wait()

        def spread(j, carry):
            for b in range(slots // 2):
                pair = stage[j, :, b * LANES : (b + 1) * LANES]
                turned = jnp.concatenate([pair[:, edge:], pair[:, :edge]], axis=1)
                twice[j * slots + 2 * b] = jnp.where(low, pair, turned)
                twice[j * slots + 2 * b + 1] = jnp.where(low, turned, pair)
            return carry

        lax.fori_loop(g * per_copy, (g + 1) * per_copy, spread, 0)
    row_copy.wait()
    pl.semaphore_wait(barrier, 1)

    def swap(i):
        return pltpu.make_async_remote_copy(
            src_ref=send.at[i],
            dst_ref=recv.at[i],
            send_sem=send_sem.at[i],
            recv_sem=recv_sem.at[i],
            device_id=other,
            device_id_type=MESH,
        )

    def one_row(i, carry):
        a = rows[i]
        for side, target in ((1, send), (0, own)):
            for o in range(half):
                for p in range(slots // 2):
                    at = (side * half + o) * slots + 2 * p
                    first = twice[picks[i, at]]
                    second = twice[picks[i, at + 1]]
                    chosen[side, o * edge : (o + 1) * edge, p * LANES : (p + 1) * LANES] = jnp.where(
                        low, first, second
                    )
            target[i] = lax.dot_general(
                a, chosen[side], (((1,), (1,)), ((), ())), preferred_element_type=jnp.float32
            )
            if side == 1:

                @pl.when(i > 0)
                def _():
                    swap(i - 1).start()

        return carry

    lax.fori_loop(0, n_rows, one_row, 0)
    swap(n_rows - 1).start()

    def finish(i, carry):
        swap(i).wait_recv()
        out[i, 0] = (own[i] + recv[i]).astype(out.dtype)
        return carry

    lax.fori_loop(0, n_rows, finish, 0)

    def drain(i, carry):
        swap(i).wait_send()
        return carry

    lax.fori_loop(0, n_rows, drain, 0)


def product(picks, rowv, colv, half):
    n_rows, edge, width = rowv.shape
    slots = width // edge
    groups = 8
    dma = pltpu.SemaphoreType.DMA
    share = (n_rows, edge, half * edge)
    return pl.pallas_call(
        product_kernel,
        name="pick_multiply_swap",
        out_shape=jax.ShapeDtypeStruct((n_rows, 1, edge, half * edge), rowv.dtype),
        in_specs=[
            pl.BlockSpec(memory_space=pltpu.SMEM),
            pl.BlockSpec(memory_space=pl.ANY),
            pl.BlockSpec(memory_space=pl.ANY),
        ],
        out_specs=pl.BlockSpec(memory_space=pltpu.VMEM),
        scratch_shapes=[
            pltpu.VMEM((n_rows, edge, width), rowv.dtype),
            pltpu.VMEM((COLS, edge, width), rowv.dtype),
            pltpu.VMEM((COLS * slots + 1, edge, LANES), rowv.dtype),
            pltpu.VMEM((2, half * edge, width), rowv.dtype),
            pltpu.VMEM(share, jnp.float32),
            pltpu.VMEM(share, jnp.float32),
            pltpu.VMEM(share, jnp.float32),
            dma(()),
            dma((groups,)),
            dma((n_rows,)),
            dma((n_rows,)),
        ],
        compiler_params=pltpu.CompilerParams(collective_id=1, has_side_effects=True),
    )(picks, rowv, colv)


def pick_table(row_cols, col_cols, targets):
    slots = row_cols.shape[1]
    count = col_cols.shape[0] * slots
    at = jnp.arange(count, dtype=jnp.int32)
    same = (targets[:, :, None, None] == (at // slots)[None, None, None, :]) & (
        row_cols[:, None, :, None] == col_cols.reshape(-1)[None, None, None, :]
    )
    found = count + jnp.sum(jnp.where(same, at - count, 0), axis=-1)
    return found.reshape(row_cols.shape[0], -1)


def per_device(p_vals, p_cols, c_cols):
    slots = p_cols.shape[1]
    half = c_cols.shape[2] // 2
    wanted = c_cols[:, 0, :] // ROWS
    targets = jnp.where(lax.axis_index("layer") == 0, wanted, jnp.roll(wanted, half, axis=1))
    padded = jnp.pad(p_cols[:, None, :], ((0, 0), (0, 0), (0, LANES - slots)))
    colv, colc, rowv, rowc = gather(p_vals, padded)
    picks = pick_table(rowc[:, 0, :slots], colc[:, 0, :slots], targets)
    return product(picks, rowv, colv, half)


def solution(mesh):
    return jax.shard_map(
        per_device,
        mesh=mesh,
        in_specs=(
            P(("prow", "pcol"), None, "layer"),
            P(("prow", "pcol"), "layer"),
            P("prow", "pcol", None),
        ),
        out_specs=P("prow", "pcol", None, "layer"),
        check_vma=False,
    )
```

```python
import jax
import jax.numpy as jnp
from jax import lax
from jax.experimental import pallas as pl
from jax.experimental.pallas import tpu as pltpu
from jax.sharding import PartitionSpec as P

MESH = pl.DeviceIdType.MESH
NX, NZ, NY, NH = 8, 4, 8, 2
COLS, ROWS = NX * NZ, NY * NH
LANES = 128
TAIL = 16


def gather_kernel(vals, cols, colv, colc, rowv, rowc, a_send, a_recv, b_send, b_recv, own_sem, t_send, t_recv):
    me_p = lax.axis_index("prow")
    me_q = lax.axis_index("pcol")
    x, z = me_p // NZ, me_p % NZ
    y, h = me_q // NH, me_q % NH
    peer_z = (z, z + 1 - 2 * (z % 2), (z + 2) % NZ, NZ - 1 - z)

    def on_p(dx, q):
        return (x + dx + NX) % NX * NZ + peer_z[q]

    def on_q(dy, p):
        return (y + dy + NY) % NY * NH + (h + p) % NH

    barrier = pltpu.get_barrier_semaphore()
    partners = [{"prow": on_p(0, k)} for k in range(1, NZ)]
    partners += [{"prow": on_p(1, 0)}, {"prow": on_p(-1, 0)}]
    partners += [{"pcol": on_q(1, 0)}, {"pcol": on_q(-1, 0)}]
    partners += [{"prow": on_p(0, k), "pcol": on_q(0, 1)} for k in range(NZ)]
    for who in partners:
        pl.semaphore_signal(barrier, inc=1, device_id=who, device_id_type=MESH)
    pl.semaphore_wait(barrier, len(partners))

    def copies(pairs, sends, recvs, sid, who):
        return [
            pltpu.make_async_remote_copy(
                src_ref=src,
                dst_ref=dst,
                send_sem=sends.at[k, sid],
                recv_sem=recvs.at[k, sid],
                device_id=who,
                device_id_type=MESH,
            )
            for k, (src, dst) in enumerate(pairs)
        ]

    sent = []

    head = pl.ds(0, vals.shape[1] - TAIL)
    tail = pl.ds(vals.shape[1] - TAIL, TAIL)

    def copies_a(slot, own, sid, who, part):
        src_c, src_v = (cols.at[0], vals.at[0]) if own else (colc.at[slot], colv.at[slot])
        dst_v = colv.at[slot]
        if part:
            src_v, dst_v = src_v.at[head], dst_v.at[head]
        return copies(((src_c, colc.at[slot]), (src_v, dst_v)), a_send, a_recv, sid, {"prow": who})

    def tail_copy(dx, q, slot):
        k = (dx - 1) * (NZ - 1) + q - 1
        return pltpu.make_async_remote_copy(
            src_ref=colv.at[slot, tail],
            dst_ref=colv.at[slot, tail],
            send_sem=t_send.at[k],
            recv_sem=t_recv.at[k],
            device_id={"prow": on_p(0, q)},
            device_id_type=MESH,
        )

    def spread_tail(dx):
        for q in range(1, NZ):
            c = tail_copy(dx, q, on_p(dx, 0))
            c.start()
            sent.append(c)

    def copies_b(slot, own, sid, who):
        src_c, src_v = (cols.at[0], vals.at[0]) if own else (rowc.at[slot], rowv.at[slot])
        return copies(((src_c, rowc.at[slot]), (src_v, rowv.at[slot])), b_send, b_recv, sid, {"pcol": who})

    def send_a(slot, own, sid, who, part=False):
        for c in copies_a(slot, own, sid, who, part):
            c.start()
            sent.append(c)

    def send_b(slot, own, sid, who):
        for c in copies_b(slot, own, sid, who):
            c.start()
            sent.append(c)

    def recv_a(slot, sid, part=False):
        for c in copies_a(slot, False, sid, on_p(1, 0), part):
            c.wait_recv()

    def recv_b(slot, sid):
        for c in copies_b(slot, False, sid, on_q(1, 0)):
            c.wait_recv()

    half_x, half_y = NX // 2, NY // 2

    def a_id(way, d, q):
        return NZ + (way * half_x + d - 1) * NZ + q

    def b_id(way, d, p):
        return 1 + (way * half_y + d - 1) * NH + p

    def goes_a(way, d, q):
        return d < half_x or (q >= NZ // 2) == (way == 1)

    def goes_b(way, d, p):
        return d < half_y or p == way

    def forward_a(way, d, q, own=False):
        if goes_a(way, d + 1, q) and d < half_x:
            step = -1 if way else 1
            send_a(on_p(-step * d, q), own, a_id(way, d + 1, q), on_p(step, 0), q > 0)

    def forward_b(way, d, p, own=False):
        if goes_b(way, d + 1, p) and d < half_y:
            step = -1 if way else 1
            send_b(on_q(-step * d, p), own, b_id(way, d + 1, p), on_q(step, 0))

    def take_a(d, q):
        if d == 0:
            recv_a(on_p(0, q), q)
        for way in (0, 1):
            if d > 0 and goes_a(way, d, q):
                recv_a(on_p(d if way else -d, q), a_id(way, d, q), q > 0)
                forward_a(way, d, q)
                if q == 0:
                    spread_tail(d if way else NX - d)
            if d == 0:
                forward_a(way, 0, q)

    def take_b(d, p):
        if d == 0:
            recv_b(on_q(0, 1), 0)
        for way in (0, 1):
            if d > 0 and goes_b(way, d, p):
                recv_b(on_q(d if way else -d, p), b_id(way, d, p))
                forward_b(way, d, p)
            if d == 0:
                forward_b(way, 0, p)

    edge = z % (NZ - 1) == 0

    def cross(q):
        @pl.when(edge)
        def _():
            for k, (src, dst) in enumerate(
                ((colc.at[on_p(0, q)], rowc.at[me_q]), (colv.at[on_p(0, q)], rowv.at[me_q]))
            ):
                cross_copy(q, k, src, dst).start()

    def cross_copy(q, k, src, dst):
        return pltpu.make_async_remote_copy(
            src_ref=src,
            dst_ref=dst,
            send_sem=own_sem.at[4 + 2 * (q - 2) + k],
            recv_sem=b_recv.at[k, 0],
            device_id={"prow": on_p(0, q), "pcol": on_q(0, 1)},
            device_id_type=MESH,
        )

    for q in range(1, NZ):
        send_a(me_p, True, q, on_p(0, q))
    for way in (0, 1):
        forward_a(way, 0, 0, True)
        forward_b(way, 0, 0, True)
    own_copies = [
        pltpu.make_async_copy(vals.at[0], colv.at[me_p], own_sem.at[0]),
        pltpu.make_async_copy(cols.at[0], colc.at[me_p], own_sem.at[1]),
        pltpu.make_async_copy(vals.at[0], rowv.at[me_q], own_sem.at[2]),
        pltpu.make_async_copy(cols.at[0], rowc.at[me_q], own_sem.at[3]),
    ]
    for c in own_copies:
        c.start()

    take_a(1, 0)
    take_b(1, 0)
    take_a(0, 1)
    take_a(2, 0)
    take_b(2, 0)
    take_a(0, 2)
    cross(2)
    take_a(1, 1)
    take_a(0, 3)
    cross(3)
    take_a(1, 2)
    take_a(2, 1)
    take_b(3, 0)
    take_b(0, 1)
    take_a(3, 0)
    take_a(1, 3)
    take_b(1, 1)
    take_b(4, 0)
    take_a(2, 2)
    take_a(3, 1)
    take_b(2, 1)
    take_a(2, 3)
    take_a(4, 0)
    take_a(3, 2)
    take_b(3, 1)
    take_a(4, 1)
    take_a(3, 3)
    take_a(4, 2)
    take_b(4, 1)
    take_a(4, 3)
    for dx in range(1, NX):
        for q in range(1, NZ):
            tail_copy(dx, q, on_p(dx, q)).wait_recv()
    for c in own_copies:
        c.wait()
    for c in sent:
        c.wait_send()

    @pl.when(edge)
    def _():
        for q in (2, 3):
            for k, (src, dst) in enumerate(
                ((colc.at[on_p(0, q)], rowc.at[me_q]), (colv.at[on_p(0, q)], rowv.at[me_q]))
            ):
                cross_copy(q, k, src, dst).wait_send()


def gather(vals, cols):
    n_a = NZ + NX * NZ
    n_b = 1 + NY * NH
    n_t = (NX - 1) * (NZ - 1)
    dma = pltpu.SemaphoreType.DMA
    shape = vals.shape[1:]
    return pl.pallas_call(
        gather_kernel,
        name="gather_both",
        out_shape=(
            jax.ShapeDtypeStruct((COLS,) + shape, vals.dtype),
            jax.ShapeDtypeStruct((COLS, 1, LANES), jnp.int32),
            jax.ShapeDtypeStruct((ROWS,) + shape, vals.dtype),
            jax.ShapeDtypeStruct((ROWS, 1, LANES), jnp.int32),
        ),
        in_specs=[pl.BlockSpec(memory_space=pltpu.VMEM)] * 2,
        out_specs=[pl.BlockSpec(memory_space=pl.ANY)] * 4,
        scratch_shapes=[dma((2, n_a)), dma((2, n_a)), dma((2, n_b)), dma((2, n_b)), dma((8,)), dma((n_t,)), dma((n_t,))],
        compiler_params=pltpu.CompilerParams(collective_id=0, has_side_effects=True),
    )(vals, cols)


def product_kernel(
    picks, rowv, colv, out, rows, stage, twice, chosen, own, send, recv, row_sem, col_sem, send_sem, recv_sem
):
    n_rows, edge, width = rows.shape
    slots = width // edge
    per_copy = COLS // col_sem.shape[0]
    groups = col_sem.shape[0]
    half = own.shape[2] // edge
    me = lax.axis_index("layer")
    other = {"layer": 1 - me}

    row_copy = pltpu.make_async_copy(rowv, rows, row_sem)
    col_copies = [
        pltpu.make_async_copy(
            colv.at[pl.ds(g * per_copy, per_copy)], stage.at[pl.ds(g * per_copy, per_copy)], col_sem.at[g]
        )
        for g in range(groups)
    ]
    for c in col_copies:
        c.start()
    row_copy.start()
    barrier = pltpu.get_barrier_semaphore()
    pl.semaphore_signal(barrier, inc=1, device_id=other, device_id_type=MESH)
    low = lax.broadcasted_iota(jnp.int32, (edge, LANES), 1) < edge
    twice[COLS * slots] = jnp.zeros((edge, LANES), twice.dtype)
    for g in range(groups):
        col_copies[g].wait()

        def spread(j, carry):
            for b in range(slots // 2):
                pair = stage[j, :, b * LANES : (b + 1) * LANES]
                turned = jnp.concatenate([pair[:, edge:], pair[:, :edge]], axis=1)
                twice[j * slots + 2 * b] = jnp.where(low, pair, turned)
                twice[j * slots + 2 * b + 1] = jnp.where(low, turned, pair)
            return carry

        lax.fori_loop(g * per_copy, (g + 1) * per_copy, spread, 0)
    row_copy.wait()
    pl.semaphore_wait(barrier, 1)

    def swap(i):
        return pltpu.make_async_remote_copy(
            src_ref=send.at[i],
            dst_ref=recv.at[i],
            send_sem=send_sem.at[i],
            recv_sem=recv_sem.at[i],
            device_id=other,
            device_id_type=MESH,
        )

    def one_row(i, carry):
        a = rows[i]
        for side, target in ((1, send), (0, own)):
            for o in range(half):
                for p in range(slots // 2):
                    at = (side * half + o) * slots + 2 * p
                    first = twice[picks[i, at]]
                    second = twice[picks[i, at + 1]]
                    chosen[side, o * edge : (o + 1) * edge, p * LANES : (p + 1) * LANES] = jnp.where(
                        low, first, second
                    )
            target[i] = lax.dot_general(
                a, chosen[side], (((1,), (1,)), ((), ())), preferred_element_type=jnp.float32
            )
            if side == 1:

                @pl.when(i > 0)
                def _():
                    swap(i - 1).start()

        return carry

    lax.fori_loop(0, n_rows, one_row, 0)
    swap(n_rows - 1).start()

    def finish(i, carry):
        swap(i).wait_recv()
        out[i, 0] = (own[i] + recv[i]).astype(out.dtype)
        return carry

    lax.fori_loop(0, n_rows, finish, 0)

    def drain(i, carry):
        swap(i).wait_send()
        return carry

    lax.fori_loop(0, n_rows, drain, 0)


def product(picks, rowv, colv, half):
    n_rows, edge, width = rowv.shape
    slots = width // edge
    groups = 8
    dma = pltpu.SemaphoreType.DMA
    share = (n_rows, edge, half * edge)
    return pl.pallas_call(
        product_kernel,
        name="pick_multiply_swap",
        out_shape=jax.ShapeDtypeStruct((n_rows, 1, edge, half * edge), rowv.dtype),
        in_specs=[
            pl.BlockSpec(memory_space=pltpu.SMEM),
            pl.BlockSpec(memory_space=pl.ANY),
            pl.BlockSpec(memory_space=pl.ANY),
        ],
        out_specs=pl.BlockSpec(memory_space=pltpu.VMEM),
        scratch_shapes=[
            pltpu.VMEM((n_rows, edge, width), rowv.dtype),
            pltpu.VMEM((COLS, edge, width), rowv.dtype),
            pltpu.VMEM((COLS * slots + 1, edge, LANES), rowv.dtype),
            pltpu.VMEM((2, half * edge, width), rowv.dtype),
            pltpu.VMEM(share, jnp.float32),
            pltpu.VMEM(share, jnp.float32),
            pltpu.VMEM(share, jnp.float32),
            dma(()),
            dma((groups,)),
            dma((n_rows,)),
            dma((n_rows,)),
        ],
        compiler_params=pltpu.CompilerParams(collective_id=1, has_side_effects=True),
    )(picks, rowv, colv)


def pick_table(row_cols, col_cols, targets):
    slots = row_cols.shape[1]
    count = col_cols.shape[0] * slots
    at = jnp.arange(count, dtype=jnp.int32)
    same = (targets[:, :, None, None] == (at // slots)[None, None, None, :]) & (
        row_cols[:, None, :, None] == col_cols.reshape(-1)[None, None, None, :]
    )
    found = count + jnp.sum(jnp.where(same, at - count, 0), axis=-1)
    return found.reshape(row_cols.shape[0], -1)


def per_device(p_vals, p_cols, c_cols):
    slots = p_cols.shape[1]
    half = c_cols.shape[2] // 2
    wanted = c_cols[:, 0, :] // ROWS
    targets = jnp.where(lax.axis_index("layer") == 0, wanted, jnp.roll(wanted, half, axis=1))
    padded = jnp.pad(p_cols[:, None, :], ((0, 0), (0, 0), (0, LANES - slots)))
    colv, colc, rowv, rowc = gather(p_vals, padded)
    picks = pick_table(rowc[:, 0, :slots], colc[:, 0, :slots], targets)
    return product(picks, rowv, colv, half)


def solution(mesh):
    return jax.shard_map(
        per_device,
        mesh=mesh,
        in_specs=(
            P(("prow", "pcol"), None, "layer"),
            P(("prow", "pcol"), "layer"),
            P("prow", "pcol", None),
        ),
        out_specs=P("prow", "pcol", None, "layer"),
        check_vma=False,
    )
```

```python
import jax
import jax.numpy as jnp
from jax import lax
from jax.experimental import pallas as pl
from jax.experimental.pallas import tpu as pltpu
from jax.sharding import PartitionSpec as P

MESH = pl.DeviceIdType.MESH
NX, NZ, NY, NH = 8, 4, 8, 2
COLS, ROWS = NX * NZ, NY * NH
LANES = 128
TAIL = 16


def fused_kernel(
    vals, cols, wanted, out, colv, colc, rowv, rowc, twice, near, far, found, picks, chosen, own, send, recv,
    a_send, a_recv, b_send, b_recv, own_sem, t_send, t_recv, s_send, s_recv,
):
    me_p = lax.axis_index("prow")
    me_q = lax.axis_index("pcol")
    me_l = lax.axis_index("layer")
    x, z = me_p // NZ, me_p % NZ
    y, h = me_q // NH, me_q % NH
    peer_z = (z, z + 1 - 2 * (z % 2), (z + 2) % NZ, NZ - 1 - z)
    edge_len, width = vals.shape[1:]
    slots = cols.shape[2]
    kept = wanted.shape[1]
    half = kept // 2
    low = lax.broadcasted_iota(jnp.int32, (edge_len, LANES), 1) < edge_len

    def on_p(dx, q):
        return (x + dx + NX) % NX * NZ + peer_z[q]

    def on_q(dy, p):
        return (y + dy + NY) % NY * NH + (h + p) % NH

    barrier = pltpu.get_barrier_semaphore()
    partners = [{"prow": on_p(0, k)} for k in range(1, NZ)]
    partners += [{"prow": on_p(1, 0)}, {"prow": on_p(-1, 0)}]
    partners += [{"pcol": on_q(1, 0)}, {"pcol": on_q(-1, 0)}]
    partners += [{"prow": on_p(0, k), "pcol": on_q(0, 1)} for k in range(NZ)]
    other = {"layer": 1 - me_l}
    partners += [other]
    for who in partners:
        pl.semaphore_signal(barrier, inc=1, device_id=who, device_id_type=MESH)
    pl.semaphore_wait(barrier, len(partners))

    def copies(pairs, sends, recvs, sid, who):
        return [
            pltpu.make_async_remote_copy(
                src_ref=src,
                dst_ref=dst,
                send_sem=sends.at[k, sid],
                recv_sem=recvs.at[k, sid],
                device_id=who,
                device_id_type=MESH,
            )
            for k, (src, dst) in enumerate(pairs)
        ]

    sent = []

    head = pl.ds(0, vals.shape[1] - TAIL)
    tail = pl.ds(vals.shape[1] - TAIL, TAIL)

    def copies_a(slot, own, sid, who, part):
        src_c, src_v = (cols.at[0], vals.at[0]) if own else (colc.at[slot], colv.at[slot])
        dst_v = colv.at[slot]
        if part:
            src_v, dst_v = src_v.at[head], dst_v.at[head]
            return copies(((src_v, dst_v),), a_send, a_recv, sid, {"prow": who})
        return copies(((src_v, dst_v), (src_c, colc.at[slot])), a_send, a_recv, sid, {"prow": who})

    def copies_b(slot, own, sid, who):
        src_c, src_v = (cols.at[0], vals.at[0]) if own else (rowc.at[slot], rowv.at[slot])
        return copies(((src_v, rowv.at[slot]), (src_c, rowc.at[slot])), b_send, b_recv, sid, {"pcol": who})

    def tail_copies(dx, q, slot):
        k = (dx - 1) * (NZ - 1) + q - 1
        pairs = ((colv.at[slot, tail], colv.at[slot, tail]), (colc.at[slot], colc.at[slot]))
        return copies(pairs, t_send, t_recv, k, {"prow": on_p(0, q)})

    def spread_tail(dx):
        for q in range(1, NZ):
            for c in tail_copies(dx, q, on_p(dx, 0)):
                c.start()
                sent.append(c)

    def spread(src, slot, first, count):
        mask = low[:count]

        def pair_of(b, carry):
            block = src[pl.ds(first, count), pl.ds(pl.multiple_of(b * LANES, LANES), LANES)]
            turned = jnp.concatenate([block[:, edge_len:], block[:, :edge_len]], axis=1)
            twice[slot, 2 * b, pl.ds(first, count), :] = jnp.where(mask, block, turned)
            twice[slot, 2 * b + 1, pl.ds(first, count), :] = jnp.where(mask, turned, block)
            return carry

        lax.fori_loop(0, slots // 2, pair_of, 0)

    def send_a(slot, own, sid, who, part=False):
        for c in copies_a(slot, own, sid, who, part):
            c.start()
            sent.append(c)

    def send_b(slot, own, sid, who):
        for c in copies_b(slot, own, sid, who):
            c.start()
            sent.append(c)

    def recv_a(slot, sid, part=False):
        for c in copies_a(slot, False, sid, on_p(1, 0), part):
            c.wait_recv()

    def recv_b(slot, sid):
        for c in copies_b(slot, False, sid, on_q(1, 0)):
            c.wait_recv()

    half_x, half_y = NX // 2, NY // 2

    def a_id(way, d, q):
        return NZ + (way * half_x + d - 1) * NZ + q

    def b_id(way, d, p):
        return 1 + (way * half_y + d - 1) * NH + p

    def goes_a(way, d, q):
        return d < half_x or (q >= NZ // 2) == (way == 1)

    def goes_b(way, d, p):
        return d < half_y or p == way

    def forward_a(way, d, q, own=False):
        if goes_a(way, d + 1, q) and d < half_x:
            step = -1 if way else 1
            send_a(on_p(-step * d, q), own, a_id(way, d + 1, q), on_p(step, 0), q > 0)

    def forward_b(way, d, p, own=False):
        if goes_b(way, d + 1, p) and d < half_y:
            step = -1 if way else 1
            send_b(on_q(-step * d, p), own, b_id(way, d + 1, p), on_q(step, 0))

    def take_a(d, q):
        if d == 0:
            recv_a(on_p(0, q), q)
        for way in (0, 1):
            if d > 0 and goes_a(way, d, q):
                recv_a(on_p(d if way else -d, q), a_id(way, d, q), q > 0)
                forward_a(way, d, q)
                if q == 0:
                    spread_tail(d if way else NX - d)
            if d == 0:
                forward_a(way, 0, q)
        for way in (0, 1):
            if (d > 0 and goes_a(way, d, q)) or (d == 0 and way == 0):
                slot = on_p(d if way else -d, q)
                spread(colv.at[slot], slot, 0, edge_len - TAIL if q and d else edge_len)

    def take_b(d, p):
        if d == 0:
            recv_b(on_q(0, 1), 0)
        for way in (0, 1):
            if d > 0 and goes_b(way, d, p):
                recv_b(on_q(d if way else -d, p), b_id(way, d, p))
                forward_b(way, d, p)
            if d == 0:
                forward_b(way, 0, p)

    edge = z % (NZ - 1) == 0

    def cross(q):
        @pl.when(edge)
        def _():
            for k, (src, dst) in enumerate(
                ((colv.at[on_p(0, q)], rowv.at[me_q]), (colc.at[on_p(0, q)], rowc.at[me_q]))
            ):
                cross_copy(q, k, src, dst).start()

    def cross_copy(q, k, src, dst):
        return pltpu.make_async_remote_copy(
            src_ref=src,
            dst_ref=dst,
            send_sem=own_sem.at[4 + 2 * (q - 2) + k],
            recv_sem=b_recv.at[k, 0],
            device_id={"prow": on_p(0, q), "pcol": on_q(0, 1)},
            device_id_type=MESH,
        )

    for q in range(1, NZ):
        send_a(me_p, True, q, on_p(0, q))
    for way in (0, 1):
        forward_a(way, 0, 0, True)
        forward_b(way, 0, 0, True)
    own_copies = [
        pltpu.make_async_copy(cols.at[0], colc.at[me_p], own_sem.at[1]),
        pltpu.make_async_copy(vals.at[0], rowv.at[me_q], own_sem.at[2]),
        pltpu.make_async_copy(cols.at[0], rowc.at[me_q], own_sem.at[3]),
    ]
    for c in own_copies:
        c.start()
    for j in range(COLS):
        twice[j, slots] = jnp.zeros((edge_len, LANES), twice.dtype)
    near[...] = jnp.zeros_like(near)
    far[...] = jnp.zeros_like(far)
    spread(vals.at[0], me_p, 0, edge_len)

    take_a(1, 0)
    take_b(1, 0)
    take_a(0, 1)
    take_a(2, 0)
    take_b(2, 0)
    take_a(0, 2)
    cross(2)
    take_a(1, 1)
    take_a(0, 3)
    cross(3)
    take_a(1, 2)
    take_a(2, 1)
    take_b(3, 0)
    take_b(0, 1)
    take_a(3, 0)
    take_a(1, 3)
    take_b(1, 1)
    take_b(4, 0)
    take_a(2, 2)
    take_a(3, 1)
    take_b(2, 1)
    take_a(2, 3)
    take_a(4, 0)
    take_a(3, 2)
    take_b(3, 1)
    take_a(3, 3)
    take_a(4, 1)
    for c in own_copies:
        c.wait()
    take_b(4, 1)
    for dx in range(1, NX):
        for q in range(1, NZ):
            slot = on_p(dx, q)
            for c in tail_copies(dx, q, slot):
                c.wait_recv()
            spread(colv.at[slot], slot, edge_len - TAIL, TAIL)

    def target(i, side, o):
        return lax.div(wanted[i, (me_l + side) % 2 * half + o], ROWS)

    def line_up(i, carry):
        for side in (0, 1):
            for o in range(half):
                r = i * kept + side * half + o
                far[pl.ds(r, 1), pl.ds(0, slots)] = colc[target(i, side, o)]
                near[pl.ds(r, 1), pl.ds(0, slots)] = rowc[i]
        return carry

    n_rows = rowv.shape[0]
    lax.fori_loop(0, n_rows, line_up, 0)
    here, there = near[...], far[...]
    which = jnp.full(here.shape, slots, jnp.int32)
    for b in range(slots):
        which = jnp.where(there[:, b : b + 1] == here, b, which)
    found[...] = which
    to_scalars = pltpu.make_async_copy(found, picks, own_sem.at[0])
    to_scalars.start()
    take_a(4, 2)
    take_a(4, 3)
    to_scalars.wait()

    def swap(i):
        return pltpu.make_async_remote_copy(
            src_ref=send.at[i],
            dst_ref=recv.at[i],
            send_sem=s_send.at[i],
            recv_sem=s_recv.at[i],
            device_id=other,
            device_id_type=MESH,
        )

    def one_row(i, carry):
        a = rowv[i]
        for side, into in ((1, send), (0, own)):
            for o in range(half):
                r = i * kept + side * half + o
                t = target(i, side, o)
                for p in range(slots // 2):
                    first = twice[t, picks[r, 2 * p]]
                    second = twice[t, picks[r, 2 * p + 1]]
                    chosen[side, o * edge_len : (o + 1) * edge_len, p * LANES : (p + 1) * LANES] = jnp.where(
                        low, first, second
                    )
            into[i] = lax.dot_general(
                a, chosen[side], (((1,), (1,)), ((), ())), preferred_element_type=jnp.float32
            )
            if side == 1:

                @pl.when(i > 0)
                def _():
                    swap(i - 1).start()

        return carry

    lax.fori_loop(0, n_rows, one_row, 0)
    swap(n_rows - 1).start()

    def finish(i, carry):
        swap(i).wait_recv()
        out[i, 0] = (own[i] + recv[i]).astype(out.dtype)
        return carry

    lax.fori_loop(0, n_rows, finish, 0)

    def drain(i, carry):
        swap(i).wait_send()
        return carry

    lax.fori_loop(0, n_rows, drain, 0)
    for c in sent:
        c.wait_send()

    @pl.when(edge)
    def _():
        for q in (2, 3):
            for k, (src, dst) in enumerate(
                ((colv.at[on_p(0, q)], rowv.at[me_q]), (colc.at[on_p(0, q)], rowc.at[me_q]))
            ):
                cross_copy(q, k, src, dst).wait_send()


def fused(vals, cols, wanted):
    n_a = NZ + NX * NZ
    n_b = 1 + NY * NH
    n_t = (NX - 1) * (NZ - 1)
    dma = pltpu.SemaphoreType.DMA
    edge_len, width = vals.shape[1:]
    slots = cols.shape[2]
    n_rows, kept = wanted.shape
    half = kept // 2
    share = (n_rows, edge_len, half * edge_len)
    return pl.pallas_call(
        fused_kernel,
        name="gather_pick_multiply_swap",
        out_shape=jax.ShapeDtypeStruct((n_rows, 1, edge_len, half * edge_len), vals.dtype),
        in_specs=[
            pl.BlockSpec(memory_space=pltpu.VMEM),
            pl.BlockSpec(memory_space=pltpu.VMEM),
            pl.BlockSpec(memory_space=pltpu.SMEM),
        ],
        out_specs=pl.BlockSpec(memory_space=pltpu.VMEM),
        scratch_shapes=[
            pltpu.VMEM((COLS, edge_len, width), vals.dtype),
            pltpu.VMEM((COLS, 1, slots), jnp.int32),
            pltpu.VMEM((ROWS, edge_len, width), vals.dtype),
            pltpu.VMEM((ROWS, 1, slots), jnp.int32),
            pltpu.VMEM((COLS, slots + 1, edge_len, LANES), vals.dtype),
            pltpu.VMEM((n_rows * kept, LANES), jnp.int32),
            pltpu.VMEM((n_rows * kept, LANES), jnp.int32),
            pltpu.VMEM((n_rows * kept, LANES), jnp.int32),
            pltpu.SMEM((n_rows * kept, LANES), jnp.int32),
            pltpu.VMEM((2, half * edge_len, width), vals.dtype),
            pltpu.VMEM(share, jnp.float32),
            pltpu.VMEM(share, jnp.float32),
            pltpu.VMEM(share, jnp.float32),
            dma((2, n_a)),
            dma((2, n_a)),
            dma((2, n_b)),
            dma((2, n_b)),
            dma((8,)),
            dma((2, n_t)),
            dma((2, n_t)),
            dma((n_rows,)),
            dma((n_rows,)),
        ],
        compiler_params=pltpu.CompilerParams(collective_id=0, has_side_effects=True),
    )(vals, cols, wanted)


def per_device(p_vals, p_cols, c_cols):
    return fused(p_vals, p_cols[:, None, :], c_cols[:, 0, :])


def solution(mesh):
    return jax.shard_map(
        per_device,
        mesh=mesh,
        in_specs=(
            P(("prow", "pcol"), None, "layer"),
            P(("prow", "pcol"), "layer"),
            P("prow", "pcol", None),
        ),
        out_specs=P("prow", "pcol", None, "layer"),
        check_vma=False,
    )
```

```python
import jax
import jax.numpy as jnp
from jax import lax
from jax.experimental import pallas as pl
from jax.experimental.pallas import tpu as pltpu
from jax.sharding import PartitionSpec as P

MESH = pl.DeviceIdType.MESH
NX, NZ, NY, NH = 8, 4, 8, 2
COLS, ROWS = NX * NZ, NY * NH
LANES = 128
TAIL = 16


def fused_kernel(
    vals, cols, wanted, out, colv, colc, rowv, rowc, twice, near, far, found, picks, chosen, own, send, recv,
    a_send, a_recv, b_send, b_recv, own_sem, t_send, t_recv, s_send, s_recv,
):
    me_p = lax.axis_index("prow")
    me_q = lax.axis_index("pcol")
    me_l = lax.axis_index("layer")
    x, z = me_p // NZ, me_p % NZ
    y, h = me_q // NH, me_q % NH
    peer_z = (z, z + 1 - 2 * (z % 2), (z + 2) % NZ, NZ - 1 - z)
    edge_len, width = vals.shape[1:]
    slots = cols.shape[2]
    kept = wanted.shape[0]
    half = kept // 2
    low = lax.broadcasted_iota(jnp.int32, (edge_len, LANES), 1) < edge_len

    def on_p(dx, q):
        return (x + dx + NX) % NX * NZ + peer_z[q]

    def on_q(dy, p):
        return (y + dy + NY) % NY * NH + (h + p) % NH

    barrier = pltpu.get_barrier_semaphore()
    partners = [{"prow": on_p(0, k)} for k in range(1, NZ)]
    partners += [{"prow": on_p(1, 0)}, {"prow": on_p(-1, 0)}]
    partners += [{"pcol": on_q(1, 0)}, {"pcol": on_q(-1, 0)}]
    partners += [{"prow": on_p(0, k), "pcol": on_q(0, 1)} for k in range(NZ)]
    other = {"layer": 1 - me_l}
    partners += [other]
    for who in partners:
        pl.semaphore_signal(barrier, inc=1, device_id=who, device_id_type=MESH)
    pl.semaphore_wait(barrier, len(partners))

    def copies(pairs, sends, recvs, sid, who):
        return [
            pltpu.make_async_remote_copy(
                src_ref=src,
                dst_ref=dst,
                send_sem=sends.at[k, sid],
                recv_sem=recvs.at[k, sid],
                device_id=who,
                device_id_type=MESH,
            )
            for k, (src, dst) in enumerate(pairs)
        ]

    sent = []

    head = pl.ds(0, vals.shape[1] - TAIL)
    tail = pl.ds(vals.shape[1] - TAIL, TAIL)

    def copies_a(slot, own, sid, who, part):
        src_c, src_v = (cols.at[0], vals.at[0]) if own else (colc.at[slot], colv.at[slot])
        dst_v = colv.at[slot]
        if part:
            src_v, dst_v = src_v.at[head], dst_v.at[head]
            return copies(((src_v, dst_v),), a_send, a_recv, sid, {"prow": who})
        return copies(((src_v, dst_v), (src_c, colc.at[slot])), a_send, a_recv, sid, {"prow": who})

    def copies_b(slot, own, sid, who):
        src_c, src_v = (cols.at[0], vals.at[0]) if own else (rowc.at[slot], rowv.at[slot])
        return copies(((src_v, rowv.at[slot]), (src_c, rowc.at[slot])), b_send, b_recv, sid, {"pcol": who})

    def tail_copies(dx, q, slot):
        k = (dx - 1) * (NZ - 1) + q - 1
        pairs = ((colv.at[slot, tail], colv.at[slot, tail]), (colc.at[slot], colc.at[slot]))
        return copies(pairs, t_send, t_recv, k, {"prow": on_p(0, q)})

    def spread_tail(dx):
        for q in range(1, NZ):
            for c in tail_copies(dx, q, on_p(dx, 0)):
                c.start()
                sent.append(c)

    def spread(j, carry):
        for b in range(slots // 2):
            block = colv[j, :, b * LANES : (b + 1) * LANES]
            turned = jnp.concatenate([block[:, edge_len:], block[:, :edge_len]], axis=1)
            twice[j, 2 * b] = jnp.where(low, block, turned)
            twice[j, 2 * b + 1] = jnp.where(low, turned, block)
        return carry

    def send_a(slot, own, sid, who, part=False):
        for c in copies_a(slot, own, sid, who, part):
            c.start()
            sent.append(c)

    def send_b(slot, own, sid, who):
        for c in copies_b(slot, own, sid, who):
            c.start()
            sent.append(c)

    def recv_a(slot, sid, part=False):
        for c in copies_a(slot, False, sid, on_p(1, 0), part):
            c.wait_recv()

    def recv_b(slot, sid):
        for c in copies_b(slot, False, sid, on_q(1, 0)):
            c.wait_recv()

    half_x, half_y = NX // 2, NY // 2

    def a_id(way, d, q):
        return NZ + (way * half_x + d - 1) * NZ + q

    def b_id(way, d, p):
        return 1 + (way * half_y + d - 1) * NH + p

    def goes_a(way, d, q):
        return d < half_x or (q >= NZ // 2) == (way == 1)

    def goes_b(way, d, p):
        return d < half_y or p == way

    def forward_a(way, d, q, own=False):
        if goes_a(way, d + 1, q) and d < half_x:
            step = -1 if way else 1
            send_a(on_p(-step * d, q), own, a_id(way, d + 1, q), on_p(step, 0), q > 0)

    def forward_b(way, d, p, own=False):
        if goes_b(way, d + 1, p) and d < half_y:
            step = -1 if way else 1
            send_b(on_q(-step * d, p), own, b_id(way, d + 1, p), on_q(step, 0))

    def take_a(d, q):
        if d == 0:
            recv_a(on_p(0, q), q)
        for way in (0, 1):
            if d > 0 and goes_a(way, d, q):
                recv_a(on_p(d if way else -d, q), a_id(way, d, q), q > 0)
                forward_a(way, d, q)
                if q == 0:
                    spread_tail(d if way else NX - d)
            if d == 0:
                forward_a(way, 0, q)

    def take_b(d, p):
        if d == 0:
            recv_b(on_q(0, 1), 0)
        for way in (0, 1):
            if d > 0 and goes_b(way, d, p):
                recv_b(on_q(d if way else -d, p), b_id(way, d, p))
                forward_b(way, d, p)
            if d == 0:
                forward_b(way, 0, p)

    edge = z % (NZ - 1) == 0

    def cross(q):
        @pl.when(edge)
        def _():
            for k, (src, dst) in enumerate(
                ((colv.at[on_p(0, q)], rowv.at[me_q]), (colc.at[on_p(0, q)], rowc.at[me_q]))
            ):
                cross_copy(q, k, src, dst).start()

    def cross_copy(q, k, src, dst):
        return pltpu.make_async_remote_copy(
            src_ref=src,
            dst_ref=dst,
            send_sem=own_sem.at[4 + 2 * (q - 2) + k],
            recv_sem=b_recv.at[k, 0],
            device_id={"prow": on_p(0, q), "pcol": on_q(0, 1)},
            device_id_type=MESH,
        )

    for q in range(1, NZ):
        send_a(me_p, True, q, on_p(0, q))
    for way in (0, 1):
        forward_a(way, 0, 0, True)
        forward_b(way, 0, 0, True)
    own_copies = [
        pltpu.make_async_copy(vals.at[0], colv.at[me_p], own_sem.at[0]),
        pltpu.make_async_copy(cols.at[0], colc.at[me_p], own_sem.at[1]),
        pltpu.make_async_copy(vals.at[0], rowv.at[me_q], own_sem.at[2]),
        pltpu.make_async_copy(cols.at[0], rowc.at[me_q], own_sem.at[3]),
    ]
    for c in own_copies:
        c.start()
    for j in range(COLS):
        twice[j, slots] = jnp.zeros((edge_len, LANES), twice.dtype)
    near[...] = jnp.zeros_like(near)
    far[...] = jnp.zeros_like(far)

    take_a(1, 0)
    take_b(1, 0)
    take_a(0, 1)
    take_a(2, 0)
    take_b(2, 0)
    take_a(0, 2)
    cross(2)
    take_a(1, 1)
    take_a(0, 3)
    cross(3)
    take_a(1, 2)
    take_a(2, 1)
    take_b(3, 0)
    take_b(0, 1)
    take_a(3, 0)
    take_a(1, 3)
    take_b(1, 1)
    take_b(4, 0)
    take_a(2, 2)
    take_a(3, 1)
    take_b(2, 1)
    take_a(2, 3)
    take_a(4, 0)
    take_a(3, 2)
    take_b(3, 1)
    take_a(3, 3)
    take_a(4, 1)
    for c in own_copies:
        c.wait()
    take_b(4, 1)
    for dx in range(1, NX):
        for q in range(1, NZ):
            slot = on_p(dx, q)
            for c in tail_copies(dx, q, slot):
                c.wait_recv()

    def target(i, side, o):
        return lax.div(wanted[(me_l + side) % 2 * half + o, 0, i], ROWS)

    def line_up(i, carry):
        for side in (0, 1):
            for o in range(half):
                r = i * kept + side * half + o
                far[pl.ds(r, 1), pl.ds(0, slots)] = colc[target(i, side, o)]
                near[pl.ds(r, 1), pl.ds(0, slots)] = rowc[i]
        return carry

    n_rows = rowv.shape[0]
    lax.fori_loop(0, n_rows, line_up, 0)
    here, there = near[...], far[...]
    which = jnp.full(here.shape, slots, jnp.int32)
    for b in range(slots):
        which = jnp.where(there[:, b : b + 1] == here, b, which)
    found[...] = which
    to_scalars = pltpu.make_async_copy(found, picks, own_sem.at[0])
    to_scalars.start()
    take_a(4, 2)
    take_a(4, 3)
    lax.fori_loop(0, COLS, spread, 0)
    to_scalars.wait()

    def swap(i):
        return pltpu.make_async_remote_copy(
            src_ref=send.at[i],
            dst_ref=recv.at[i],
            send_sem=s_send.at[i],
            recv_sem=s_recv.at[i],
            device_id=other,
            device_id_type=MESH,
        )

    def one_row(side, into, i):
        for o in range(half):
            r = i * kept + side * half + o
            t = target(i, side, o)
            for p in range(slots // 2):
                first = twice[t, picks[r, 2 * p]]
                second = twice[t, picks[r, 2 * p + 1]]
                chosen[side, o * edge_len : (o + 1) * edge_len, p * LANES : (p + 1) * LANES] = jnp.where(
                    low, first, second
                )
        into[i] = lax.dot_general(
            rowv[i], chosen[side], (((1,), (1,)), ((), ())), preferred_element_type=jnp.float32
        )

    def send_row(i, carry):
        one_row(1, send, i)

        @pl.when(i > 0)
        def _():
            swap(i - 1).start()

        return carry

    def own_row(i, carry):
        one_row(0, own, i)
        return carry

    lax.fori_loop(0, n_rows, send_row, 0)
    swap(n_rows - 1).start()
    lax.fori_loop(0, n_rows, own_row, 0)

    def finish(i, carry):
        swap(i).wait_recv()
        out[i, 0] = (own[i] + recv[i]).astype(out.dtype)
        return carry

    lax.fori_loop(0, n_rows, finish, 0)

    def drain(i, carry):
        swap(i).wait_send()
        return carry

    lax.fori_loop(0, n_rows, drain, 0)
    for c in sent:
        c.wait_send()

    @pl.when(edge)
    def _():
        for q in (2, 3):
            for k, (src, dst) in enumerate(
                ((colv.at[on_p(0, q)], rowv.at[me_q]), (colc.at[on_p(0, q)], rowc.at[me_q]))
            ):
                cross_copy(q, k, src, dst).wait_send()


def fused(vals, cols, wanted):
    n_a = NZ + NX * NZ
    n_b = 1 + NY * NH
    n_t = (NX - 1) * (NZ - 1)
    dma = pltpu.SemaphoreType.DMA
    edge_len, width = vals.shape[1:]
    slots = cols.shape[2]
    kept, _, n_rows = wanted.shape
    half = kept // 2
    share = (n_rows, edge_len, half * edge_len)
    return pl.pallas_call(
        fused_kernel,
        name="gather_pick_multiply_swap",
        out_shape=jax.ShapeDtypeStruct((n_rows, 1, edge_len, half * edge_len), vals.dtype),
        in_specs=[
            pl.BlockSpec(memory_space=pltpu.VMEM),
            pl.BlockSpec(memory_space=pltpu.VMEM),
            pl.BlockSpec(memory_space=pltpu.SMEM),
        ],
        out_specs=pl.BlockSpec(memory_space=pltpu.VMEM),
        scratch_shapes=[
            pltpu.VMEM((COLS, edge_len, width), vals.dtype),
            pltpu.VMEM((COLS, 1, slots), jnp.int32),
            pltpu.VMEM((ROWS, edge_len, width), vals.dtype),
            pltpu.VMEM((ROWS, 1, slots), jnp.int32),
            pltpu.VMEM((COLS, slots + 1, edge_len, LANES), vals.dtype),
            pltpu.VMEM((n_rows * kept, LANES), jnp.int32),
            pltpu.VMEM((n_rows * kept, LANES), jnp.int32),
            pltpu.VMEM((n_rows * kept, LANES), jnp.int32),
            pltpu.SMEM((n_rows * kept, LANES), jnp.int32),
            pltpu.VMEM((2, half * edge_len, width), vals.dtype),
            pltpu.VMEM(share, jnp.float32),
            pltpu.VMEM(share, jnp.float32),
            pltpu.VMEM(share, jnp.float32),
            dma((2, n_a)),
            dma((2, n_a)),
            dma((2, n_b)),
            dma((2, n_b)),
            dma((8,)),
            dma((2, n_t)),
            dma((2, n_t)),
            dma((n_rows,)),
            dma((n_rows,)),
        ],
        compiler_params=pltpu.CompilerParams(collective_id=0, has_side_effects=True),
    )(vals, cols, wanted)


def per_device(p_vals, p_cols, c_cols):
    return fused(p_vals, p_cols[:, None, :], jnp.transpose(c_cols, (2, 1, 0)))


def solution(mesh):
    return jax.shard_map(
        per_device,
        mesh=mesh,
        in_specs=(
            P(("prow", "pcol"), None, "layer"),
            P(("prow", "pcol"), "layer"),
            P("prow", "pcol", None),
        ),
        out_specs=P("prow", "pcol", None, "layer"),
        check_vma=False,
    )
```

```python
import jax
import jax.numpy as jnp
from jax import lax
from jax.experimental import pallas as pl
from jax.experimental.pallas import tpu as pltpu
from jax.sharding import PartitionSpec as P

MESH = pl.DeviceIdType.MESH
NX, NZ, NY, NH = 8, 4, 8, 2
COLS, ROWS = NX * NZ, NY * NH
LANES = 128
TAIL = 16


def fused_kernel(
    vals, cols, wanted, out, colv, colc, rowv, rowc, twice, near, far, found, picks, chosen, own, send, recv,
    a_send, a_recv, b_send, b_recv, own_sem, t_send, t_recv, s_send, s_recv,
):
    me_p = lax.axis_index("prow")
    me_q = lax.axis_index("pcol")
    me_l = lax.axis_index("layer")
    x, z = me_p // NZ, me_p % NZ
    y, h = me_q // NH, me_q % NH
    peer_z = (z, z + 1 - 2 * (z % 2), (z + 2) % NZ, NZ - 1 - z)
    edge_len, width = vals.shape[1:]
    slots = cols.shape[2]
    kept = wanted.shape[0]
    half = kept // 2
    low = lax.broadcasted_iota(jnp.int32, (edge_len, LANES), 1) < edge_len

    def on_p(dx, q):
        return (x + dx + NX) % NX * NZ + peer_z[q]

    def on_q(dy, p):
        return (y + dy + NY) % NY * NH + (h + p) % NH

    barrier = pltpu.get_barrier_semaphore()
    partners = [{"prow": on_p(0, k)} for k in range(1, NZ)]
    partners += [{"prow": on_p(1, 0)}, {"prow": on_p(-1, 0)}]
    partners += [{"pcol": on_q(1, 0)}, {"pcol": on_q(-1, 0)}]
    partners += [{"prow": on_p(0, k), "pcol": on_q(0, 1)} for k in range(NZ)]
    other = {"layer": 1 - me_l}
    partners += [other]
    for who in partners:
        pl.semaphore_signal(barrier, inc=1, device_id=who, device_id_type=MESH)
    pl.semaphore_wait(barrier, len(partners))

    def copies(pairs, sends, recvs, sid, who):
        return [
            pltpu.make_async_remote_copy(
                src_ref=src,
                dst_ref=dst,
                send_sem=sends.at[k, sid],
                recv_sem=recvs.at[k, sid],
                device_id=who,
                device_id_type=MESH,
            )
            for k, (src, dst) in enumerate(pairs)
        ]

    sent = []

    head = pl.ds(0, vals.shape[1] - TAIL)
    tail = pl.ds(vals.shape[1] - TAIL, TAIL)

    def copies_a(slot, own, sid, who, part):
        src_c, src_v = (cols.at[0], vals.at[0]) if own else (colc.at[slot], colv.at[slot])
        dst_v = colv.at[slot]
        if part:
            src_v, dst_v = src_v.at[head], dst_v.at[head]
            return copies(((src_v, dst_v),), a_send, a_recv, sid, {"prow": who})
        return copies(((src_v, dst_v), (src_c, colc.at[slot])), a_send, a_recv, sid, {"prow": who})

    def copies_b(slot, own, sid, who):
        src_c, src_v = (cols.at[0], vals.at[0]) if own else (rowc.at[slot], rowv.at[slot])
        return copies(((src_v, rowv.at[slot]), (src_c, rowc.at[slot])), b_send, b_recv, sid, {"pcol": who})

    def tail_copies(dx, q, slot):
        k = (dx - 1) * (NZ - 1) + q - 1
        pairs = ((colv.at[slot, tail], colv.at[slot, tail]), (colc.at[slot], colc.at[slot]))
        return copies(pairs, t_send, t_recv, k, {"prow": on_p(0, q)})

    def spread_tail(dx):
        for q in range(1, NZ):
            for c in tail_copies(dx, q, on_p(dx, 0)):
                c.start()
                sent.append(c)

    def spread(j, carry):
        for b in range(slots // 2):
            block = colv[j, :, b * LANES : (b + 1) * LANES]
            turned = jnp.concatenate([block[:, edge_len:], block[:, :edge_len]], axis=1)
            twice[j, 2 * b] = jnp.where(low, block, turned)
            twice[j, 2 * b + 1] = jnp.where(low, turned, block)
        return carry

    def send_a(slot, own, sid, who, part=False):
        for c in copies_a(slot, own, sid, who, part):
            c.start()
            sent.append(c)

    def send_b(slot, own, sid, who):
        for c in copies_b(slot, own, sid, who):
            c.start()
            sent.append(c)

    def recv_a(slot, sid, part=False):
        for c in copies_a(slot, False, sid, on_p(1, 0), part):
            c.wait_recv()

    def recv_b(slot, sid):
        for c in copies_b(slot, False, sid, on_q(1, 0)):
            c.wait_recv()

    half_x, half_y = NX // 2, NY // 2

    def a_id(way, d, q):
        return NZ + (way * half_x + d - 1) * NZ + q

    def b_id(way, d, p):
        return 1 + (way * half_y + d - 1) * NH + p

    def goes_a(way, d, q):
        return d < half_x or (q >= NZ // 2) == (way == 1)

    def goes_b(way, d, p):
        return d < half_y or p == way

    def forward_a(way, d, q, own=False):
        if goes_a(way, d + 1, q) and d < half_x:
            step = -1 if way else 1
            send_a(on_p(-step * d, q), own, a_id(way, d + 1, q), on_p(step, 0), q > 0)

    def forward_b(way, d, p, own=False):
        if goes_b(way, d + 1, p) and d < half_y:
            step = -1 if way else 1
            send_b(on_q(-step * d, p), own, b_id(way, d + 1, p), on_q(step, 0))

    def take_a(d, q):
        if d == 0:
            recv_a(on_p(0, q), q)
        for way in (0, 1):
            if d > 0 and goes_a(way, d, q):
                recv_a(on_p(d if way else -d, q), a_id(way, d, q), q > 0)
                forward_a(way, d, q)
                if q == 0:
                    spread_tail(d if way else NX - d)
            if d == 0:
                forward_a(way, 0, q)

    def take_b(d, p):
        if d == 0:
            recv_b(on_q(0, 1), 0)
        for way in (0, 1):
            if d > 0 and goes_b(way, d, p):
                recv_b(on_q(d if way else -d, p), b_id(way, d, p))
                forward_b(way, d, p)
            if d == 0:
                forward_b(way, 0, p)

    edge = z % (NZ - 1) == 0

    def cross(q):
        @pl.when(edge)
        def _():
            for k, (src, dst) in enumerate(
                ((colv.at[on_p(0, q)], rowv.at[me_q]), (colc.at[on_p(0, q)], rowc.at[me_q]))
            ):
                cross_copy(q, k, src, dst).start()

    def cross_copy(q, k, src, dst):
        return pltpu.make_async_remote_copy(
            src_ref=src,
            dst_ref=dst,
            send_sem=own_sem.at[4 + 2 * (q - 2) + k],
            recv_sem=b_recv.at[k, 0],
            device_id={"prow": on_p(0, q), "pcol": on_q(0, 1)},
            device_id_type=MESH,
        )

    for q in range(1, NZ):
        send_a(me_p, True, q, on_p(0, q))
    for way in (0, 1):
        forward_a(way, 0, 0, True)
        forward_b(way, 0, 0, True)
    own_copies = [
        pltpu.make_async_copy(vals.at[0], colv.at[me_p], own_sem.at[0]),
        pltpu.make_async_copy(cols.at[0], colc.at[me_p], own_sem.at[1]),
        pltpu.make_async_copy(vals.at[0], rowv.at[me_q], own_sem.at[2]),
        pltpu.make_async_copy(cols.at[0], rowc.at[me_q], own_sem.at[3]),
    ]
    for c in own_copies:
        c.start()
    for j in range(COLS):
        twice[j, slots] = jnp.zeros((edge_len, LANES), twice.dtype)
    near[...] = jnp.zeros_like(near)
    far[...] = jnp.zeros_like(far)

    take_a(1, 0)
    take_b(1, 0)
    take_a(0, 1)
    take_a(2, 0)
    take_b(2, 0)
    take_a(0, 2)
    cross(2)
    take_a(1, 1)
    take_a(0, 3)
    cross(3)
    take_a(1, 2)
    take_a(2, 1)
    take_b(3, 0)
    take_b(0, 1)
    take_a(3, 0)
    take_a(1, 3)
    take_b(1, 1)
    take_b(4, 0)
    take_a(2, 2)
    take_a(3, 1)
    take_b(2, 1)
    take_a(2, 3)
    take_a(4, 0)
    take_a(3, 2)
    take_b(3, 1)
    take_a(3, 3)
    take_a(4, 1)
    for c in own_copies:
        c.wait()
    take_b(4, 1)
    for dx in range(1, NX):
        for q in range(1, NZ):
            slot = on_p(dx, q)
            for c in tail_copies(dx, q, slot):
                c.wait_recv()

    def target(i, side, o):
        return lax.div(wanted[(me_l + side) % 2 * half + o, 0, i], ROWS)

    def line_up(i, carry):
        for side in (0, 1):
            for o in range(half):
                r = i * kept + side * half + o
                far[pl.ds(r, 1), pl.ds(0, slots)] = colc[target(i, side, o)]
                near[pl.ds(r, 1), pl.ds(0, slots)] = rowc[i]
        return carry

    n_rows = rowv.shape[0]
    lax.fori_loop(0, n_rows, line_up, 0)
    here, there = near[...], far[...]
    which = jnp.full(here.shape, slots, jnp.int32)
    for b in range(slots):
        which = jnp.where(there[:, b : b + 1] == here, b, which)
    found[...] = which
    to_scalars = pltpu.make_async_copy(found, picks, own_sem.at[0])
    to_scalars.start()
    take_a(4, 2)
    take_a(4, 3)
    lax.fori_loop(0, COLS, spread, 0)
    to_scalars.wait()

    def swap(i):
        return pltpu.make_async_remote_copy(
            src_ref=send.at[i],
            dst_ref=recv.at[i],
            send_sem=s_send.at[i],
            recv_sem=s_recv.at[i],
            device_id=other,
            device_id_type=MESH,
        )

    def one_row(side, into, i, buf):
        for o in range(half):
            r = i * kept + side * half + o
            t = target(i, side, o)
            for p in range(slots // 2):
                first = twice[t, picks[r, 2 * p]]
                second = twice[t, picks[r, 2 * p + 1]]
                chosen[buf, o * edge_len : (o + 1) * edge_len, p * LANES : (p + 1) * LANES] = jnp.where(
                    low, first, second
                )
        into[i] = lax.dot_general(
            rowv[i], chosen[buf], (((1,), (1,)), ((), ())), preferred_element_type=jnp.float32
        )

    group = chosen.shape[0]

    def send_rows(g, carry):
        for k in range(group):
            one_row(1, send, g * group + k, k)

        @pl.when(g > 0)
        def _():
            for k in range(group):
                swap((g - 1) * group + k).start()

        return carry

    def own_rows(g, carry):
        for k in range(group):
            one_row(0, own, g * group + k, k)
        return carry

    lax.fori_loop(0, n_rows // group, send_rows, 0)
    for k in range(group):
        swap(n_rows - group + k).start()
    lax.fori_loop(0, n_rows // group, own_rows, 0)

    def finish(i, carry):
        swap(i).wait_recv()
        out[i, 0] = (own[i] + recv[i]).astype(out.dtype)
        return carry

    lax.fori_loop(0, n_rows, finish, 0)

    def drain(i, carry):
        swap(i).wait_send()
        return carry

    lax.fori_loop(0, n_rows, drain, 0)
    for c in sent:
        c.wait_send()

    @pl.when(edge)
    def _():
        for q in (2, 3):
            for k, (src, dst) in enumerate(
                ((colv.at[on_p(0, q)], rowv.at[me_q]), (colc.at[on_p(0, q)], rowc.at[me_q]))
            ):
                cross_copy(q, k, src, dst).wait_send()


def fused(vals, cols, wanted):
    n_a = NZ + NX * NZ
    n_b = 1 + NY * NH
    n_t = (NX - 1) * (NZ - 1)
    dma = pltpu.SemaphoreType.DMA
    edge_len, width = vals.shape[1:]
    slots = cols.shape[2]
    kept, _, n_rows = wanted.shape
    half = kept // 2
    share = (n_rows, edge_len, half * edge_len)
    return pl.pallas_call(
        fused_kernel,
        name="gather_pick_multiply_swap",
        out_shape=jax.ShapeDtypeStruct((n_rows, 1, edge_len, half * edge_len), vals.dtype),
        in_specs=[
            pl.BlockSpec(memory_space=pltpu.VMEM),
            pl.BlockSpec(memory_space=pltpu.VMEM),
            pl.BlockSpec(memory_space=pltpu.SMEM),
        ],
        out_specs=pl.BlockSpec(memory_space=pltpu.VMEM),
        scratch_shapes=[
            pltpu.VMEM((COLS, edge_len, width), vals.dtype),
            pltpu.VMEM((COLS, 1, slots), jnp.int32),
            pltpu.VMEM((ROWS, edge_len, width), vals.dtype),
            pltpu.VMEM((ROWS, 1, slots), jnp.int32),
            pltpu.VMEM((COLS, slots + 1, edge_len, LANES), vals.dtype),
            pltpu.VMEM((n_rows * kept, LANES), jnp.int32),
            pltpu.VMEM((n_rows * kept, LANES), jnp.int32),
            pltpu.VMEM((n_rows * kept, LANES), jnp.int32),
            pltpu.SMEM((n_rows * kept, LANES), jnp.int32),
            pltpu.VMEM((4, half * edge_len, width), vals.dtype),
            pltpu.VMEM(share, jnp.float32),
            pltpu.VMEM(share, jnp.float32),
            pltpu.VMEM(share, jnp.float32),
            dma((2, n_a)),
            dma((2, n_a)),
            dma((2, n_b)),
            dma((2, n_b)),
            dma((8,)),
            dma((2, n_t)),
            dma((2, n_t)),
            dma((n_rows,)),
            dma((n_rows,)),
        ],
        compiler_params=pltpu.CompilerParams(collective_id=0, has_side_effects=True),
    )(vals, cols, wanted)


def per_device(p_vals, p_cols, c_cols):
    return fused(p_vals, p_cols[:, None, :], jnp.transpose(c_cols, (2, 1, 0)))


def solution(mesh):
    return jax.shard_map(
        per_device,
        mesh=mesh,
        in_specs=(
            P(("prow", "pcol"), None, "layer"),
            P(("prow", "pcol"), "layer"),
            P("prow", "pcol", None),
        ),
        out_specs=P("prow", "pcol", None, "layer"),
        check_vma=False,
    )
```
